32 devices in a mesh: gx: 8 (over z, x), gy: 4 (over y, core).
Axes of the slice: x: 2, y: 2, z: 4, core: 2. Of those that a mesh axis runs over, the one named last changes fastest.
Arguments:
- u_prev: float32 [3, 32, 128, 2048], P(None, None, 'gx', 'gy'), may hold values from -6 to 6
- u_now: float32 [3, 32, 128, 2048], P(None, None, 'gx', 'gy'), may hold values from -6 to 6
- speeds: float32 [2, 32, 128, 2048], P(None, None, 'gx', 'gy'), may hold values from 0.1 to 0.24
- sites: int32 [12288], P(('gx', 'gy')), may hold values from 0 to 8191
- routes: int32 [12288, 1], P(('gx', 'gy')), may hold values from 0 to 31; in each aligned block of 384 rows (0 to 383, 384 to 767, ...) at most 32 rows name the same one
- frame_disp: float32 [240, 32768], P(None, ('gx', 'gy')), may hold values from -4 to 4
- frame_vel: float32 [240, 32768], P(None, ('gx', 'gy')), may hold values from -6 to 6
- frame_acc: float32 [240, 32768], P(None, ('gx', 'gy')), may hold values from -6 to 6
- frame_hyst: float32 [240, 32768], P(None, ('gx', 'gy')), may hold values from -0.5 to 0.5
- frame_kind: int32 [32768], P(('gx', 'gy')), may hold values from 0 to 3
- stiffness: float32 [4, 240, 240], replicated, as said below
Outputs:
- field_before: float32 [3, 32, 128, 2048], P(None, None, 'gx', 'gy')
- field_last: float32 [3, 32, 128, 2048], P(None, None, 'gx', 'gy')
- disp_next: float32 [240, 32768], P(None, ('gx', 'gy'))
- vel_next: float32 [240, 32768], P(None, ('gx', 'gy'))
- acc_next: float32 [240, 32768], P(None, ('gx', 'gy'))
- hyst_next: float32 [240, 32768], P(None, ('gx', 'gy'))
The draws below stay inside these ranges and needn't reach their ends.
Inputs may be any that keep to these rules, and one draw needn't show every extreme that they name: `routes`: among the buildings of one device, no owner is named by more than 32 of them, a bound that some block reaches. `stiffness`: diagonal entries between 1 and 2; off-diagonal entries small.
All inputs are finite; a program needn't handle non-finite values.
Results may differ from the reference program's by a relative error of at most 0.00023.
Values sent between devices are 32-bit elements; how exact they have to be, the bound alone decides.
A program may use at most 192 MiB of HBM per device.

```python
import math
import jax
import jax.numpy as jnp
import numpy as np
from jax import lax

CX = 16
CY = 512
NZ = 32
STEPS = 4
NF = 240
NA = 4
B_DEV = 384
ROWS_DEV = 1024
NX = 128
NY = 2048
BUILDINGS = 12288
SLOTS = 32768
N_GX = 8
N_GY = 4
DEVICES = 32


def draw_stiffness(key, part):
    first_key, second_key = jax.random.split(jax.random.fold_in(key, 11))
    diagonal = jax.random.uniform(first_key, (NA, NF, NF), jnp.float32, 1.0, 2.0)
    off_diag = 0.03 * jax.random.normal(second_key, (NA, NF, NF), jnp.float32)
    identity = jnp.eye(NF, dtype=jnp.float32)[None, :, :]
    return jnp.where(identity > 0.5, diagonal, off_diag).astype(jnp.float32)


def checker_field(key, salt):
    mag_key, noise_key = jax.random.split(jax.random.fold_in(key, salt))
    depth_ids = jnp.arange(NZ, dtype=jnp.int32)[:, None, None]
    east_ids = jnp.arange(NX, dtype=jnp.int32)[None, :, None]
    north_ids = jnp.arange(NY, dtype=jnp.int32)[None, None, :]
    parity = ((depth_ids + east_ids + north_ids) % 2).astype(jnp.float32)
    signs = (1.0 - 2.0 * parity)[None, :, :, :]
    shape = (3, NZ, NX, NY)
    magnitude = jax.random.uniform(mag_key, shape, jnp.float32, 1.5, 4.5)
    noise = jnp.clip(0.6 * jax.random.normal(noise_key, shape, jnp.float32), -1.5, 1.5)
    return (signs * magnitude + noise).astype(jnp.float32)


def draw_u_prev(key, part):
    return checker_field(key, 23)


def draw_u_now(key, part):
    return checker_field(key, 37)


def place_ends(result, rng, least, largest):
    longest = result.shape.index(max(result.shape))
    spots = []
    for shift in (0, 1):
        where = [jax.random.randint(jax.random.fold_in(rng, axis), (), 0, length) for axis, length in enumerate(result.shape)]
        where[longest] = (where[longest] + shift) % result.shape[longest]
        spots.append(tuple(where))
    return result.at[spots[0]].set(least).at[spots[1]].set(largest)


def shard_levels(own_key, shape, cuts, smallest, largest):
    factor_of, own = 1.0, jax.random.fold_in(own_key, 6)
    for position, shards_of in cuts:
        draws = jnp.exp(jax.random.uniform(jax.random.fold_in(own, position), (shards_of,), jnp.float32, smallest / len(cuts), largest / len(cuts)))
        factor_of = factor_of * jnp.repeat(draws, shape[position] // shards_of).reshape([-1 if axis == position else 1 for axis in range(len(shape))])
    return factor_of


def deal_out(own_key, own, number, rows, amount, top, reach, skew):
    sequence = jax.random.permutation(own_key, amount)
    heavy_load, common = shares(amount, rows * top, reach, skew, True), shares(amount, rows * top, reach, skew, False)
    places = jnp.arange(amount)

    def named(tallies, turn):
        used = int((tallies > 0).sum())
        fixed = max(1, used // 4)
        shifted = fixed + (places - fixed + turn * (used - fixed)) % max(1, amount - fixed)
        return jnp.zeros((amount,), jnp.int32).at[sequence[jnp.where(places < fixed, places, shifted)]].set(jnp.asarray(tallies, jnp.int32))

    tallies = jnp.where(number % 4 == 0, named(heavy_load, number // 4), named(common, number - number // 4 - 1))
    mixed = jax.random.permutation(jax.random.fold_in(own, 3), amount)
    donor, sink = mixed[0:amount // 2 * 2:2], mixed[1:amount // 2 * 2:2]
    margin = jnp.minimum(tallies[donor] - 1, reach - tallies[sink]) // 2
    margin = jnp.where((donor == sequence[0]) | (sink == sequence[0]) | (tallies[sink] == 0), 0, jnp.maximum(margin, 0))
    shifted = jax.random.randint(jax.random.fold_in(own, 4), (amount // 2,), 0, 1 << 20) % (margin + 1)
    tallies = tallies.at[donor].add(-shifted).at[sink].add(shifted)
    items = jnp.searchsorted(jnp.cumsum(tallies), jnp.arange(rows * top), side="right").astype(jnp.int32)
    table = items.reshape(top, rows).T
    table = table[jax.random.permutation(jax.random.fold_in(own, 1), rows)]
    turn = jax.random.randint(jax.random.fold_in(own, 2), (rows, 1), 0, top)
    return jnp.take_along_axis(table, (jnp.arange(top)[None, :] + turn) % top, axis=1)


def shares(count, total, most, skew, full):
    loads = [(1 << 20) // math.isqrt(standing ** skew) + 1 for standing in range(1, count + 1)]
    largest = most if full else min(most, max(-(-total // count), total * loads[0] // sum(loads)))
    least = 1 if total - largest >= count - 1 else 0
    counts, spare = [largest] + [least] * (count - 1), total - largest - least * (count - 1)
    while spare > 0:
        movable = [i for i in range(1, count) if counts[i] < largest] or [i for i in range(1, count) if counts[i] < most]
        mass, left = sum([loads[i] for i in movable]), spare
        for i in movable:
            extra = min(most - counts[i], max(1, left * loads[i] // mass), spare)
            counts[i] = counts[i] + extra
            spare = spare - extra
    return np.array(counts)


def gaussian(own_key, extent, scale, reach, pieces=(), held_as=jnp.bfloat16):
    gain = shard_levels(own_key, extent, pieces, -0.22, 0.18) if pieces else 1.0
    values = jax.random.normal(own_key, extent, jnp.float32) * scale * gain
    return jnp.minimum(jnp.maximum(values, -reach), reach).astype(held_as)


def setup_inputs(seed: int = 0) -> dict:
    key_list = jax.random.split(jax.random.key(seed), 12)
    u_prev = draw_u_prev(jax.random.fold_in(key_list[11], 71), 0)
    u_now = draw_u_now(jax.random.fold_in(key_list[11], 71), 0)
    speeds = jnp.clip(jnp.exp(math.log(0.24) - 0.8754687 * jax.random.uniform(key_list[2], (2, NZ, NX, NY), jnp.float32) ** shard_levels(key_list[2], (2, NZ, NX, NY), ((2, 8), (3, 4)), -0.2, 0.2)), 0.1, 0.24)
    sites = place_ends(jax.random.randint(key_list[3], (BUILDINGS,), 0, CX * CY), jax.random.fold_in(key_list[3], 1), 0, (CX * CY) - 1).astype(jnp.int32)
    routes_keys = jax.random.split(jax.random.fold_in(key_list[4], 1), BUILDINGS // B_DEV)
    routes_turns = jax.random.permutation(jax.random.fold_in(key_list[4], 3), BUILDINGS // B_DEV)
    routes = jax.vmap(lambda own, number: deal_out(jax.random.fold_in(key_list[4], 2), own, number, B_DEV, DEVICES, 1, ROWS_DEV // DEVICES, 2))(routes_keys, routes_turns).reshape((BUILDINGS, 1))
    frame_disp = gaussian(key_list[5], (NF, SLOTS), 0.5, 4.0, ((1, 32),), jnp.float32)
    frame_vel = gaussian(key_list[6], (NF, SLOTS), 1.0, 6.0, ((1, 32),), jnp.float32)
    frame_acc = gaussian(key_list[7], (NF, SLOTS), 1.0, 6.0, ((1, 32),), jnp.float32)
    frame_hyst = jnp.clip(jax.random.uniform(key_list[8], (NF, SLOTS), jnp.float32, -0.5, 0.5) * shard_levels(key_list[8], (NF, SLOTS), ((1, 32),), -0.4, 0.0), -0.5, 0.5)
    frame_kind = place_ends(jax.random.randint(key_list[9], (SLOTS,), 0, NA), jax.random.fold_in(key_list[9], 1), 0, NA - 1).astype(jnp.int32)
    stiffness = draw_stiffness(jax.random.fold_in(key_list[11], 71), 0)
    return {"u_prev": u_prev, "u_now": u_now, "speeds": speeds, "sites": sites, "routes": routes, "frame_disp": frame_disp, "frame_vel": frame_vel, "frame_acc": frame_acc, "frame_hyst": frame_hyst, "frame_kind": frame_kind, "stiffness": stiffness}


time_step = 0.5
damping = 0.1
yield_drift = 0.5
hyst_stiff = 1.0
ground_gain = 0.1


def trim_rim(array, dims, width):
    for dim in dims:
        array = lax.slice_in_dim(array, width, array.shape[dim] - width, axis=dim)
    return array


def second_diff(padded, dim):
    length = padded.shape[dim]

    def part(start):
        return lax.slice_in_dim(padded, start, length - 4 + start, axis=dim)

    return (16.0 * (part(1) + part(3)) - (part(0) + part(4)) - 30.0 * part(2)) / 12.0


def wave_accel(padded, speeds):
    along_depth = trim_rim(second_diff(padded, 1), (2, 3), 2)
    along_east = trim_rim(second_diff(padded, 2), (1, 3), 2)
    along_north = trim_rim(second_diff(padded, 3), (1, 2), 2)
    own_term = jnp.stack([along_east[0], along_north[1], along_depth[2]])
    total = along_east + along_north + along_depth
    return speeds[0] * own_term + speeds[1] * (total - own_term)


def shift_down(values):
    return jnp.concatenate([jnp.zeros_like(values[:3]), values[:-3]], axis=0)


def shift_up(values):
    return jnp.concatenate([values[3:], jnp.zeros_like(values[:3])], axis=0)


def frame_step(slot_motion, frame_disp, frame_vel, frame_acc, frame_hyst, frame_kind, stiffness):
    disp_next = frame_disp + time_step * frame_vel + 0.5 * time_step * time_step * frame_acc
    drift_change = (disp_next - shift_down(disp_next)) - (frame_disp - shift_down(frame_disp))
    hyst_next = jnp.clip(frame_hyst + drift_change, -yield_drift, yield_drift)
    elastic = jnp.zeros_like(disp_next)
    for kind in range(stiffness.shape[0]):
        product = jnp.dot(stiffness[kind], disp_next, precision=lax.Precision.HIGHEST)
        elastic = elastic + jnp.where(frame_kind[None, :] == kind, product, 0.0)
    forcing = jnp.tile(slot_motion, (frame_disp.shape[0] // 3, 1))
    acc_next = (-forcing - damping * (frame_vel + 0.5 * time_step * frame_acc) - elastic
                - hyst_stiff * (hyst_next - shift_up(hyst_next)))
    vel_next = frame_vel + 0.5 * time_step * (frame_acc + acc_next)
    return disp_next, vel_next, acc_next, hyst_next


def reference(u_prev, u_now, speeds, sites, routes, frame_disp, frame_vel, frame_acc, frame_hyst, frame_kind, stiffness):
    levels = [u_prev, u_now]
    for step in range(STEPS):
        padded = jnp.pad(levels[-1], ((0, 0), (2, 2), (2, 2), (2, 2)))
        levels.append(2.0 * levels[-1] - levels[-2] + wave_accel(padded, speeds))
    ground = ground_gain * (levels[-1] - 2.0 * levels[-2] + levels[-3])[:, 0]
    devices = N_GX * N_GY
    holder = jnp.arange(devices * B_DEV, dtype=jnp.int32) // B_DEV
    row_cell = (holder // N_GY) * CX + sites // CY
    col_cell = (holder % N_GY) * CY + sites % CY
    motion = ground[:, row_cell, col_cell]
    target_dev = routes[:, 0].reshape(devices, B_DEV)
    onehot = (target_dev[:, :, None] == jnp.arange(devices, dtype=jnp.int32)[None, None, :]).astype(jnp.int32)
    before = jnp.cumsum(onehot, axis=1) - onehot
    rank = jnp.sum(before * onehot, axis=2)
    source = jnp.arange(devices, dtype=jnp.int32)[:, None]
    capacity = ROWS_DEV // devices
    target = (target_dev * ROWS_DEV + source * capacity + rank).reshape(-1).astype(jnp.int32)
    slot_motion = jnp.zeros((3, devices * ROWS_DEV), jnp.float32).at[:, target].set(motion)
    disp_next, vel_next, acc_next, hyst_next = frame_step(slot_motion, frame_disp, frame_vel, frame_acc, frame_hyst, frame_kind, stiffness)
    return levels[-2], levels[-1], disp_next, vel_next, acc_next, hyst_next
```

```python
import functools

import jax
import jax.numpy as jnp
from jax import lax
from jax.experimental import pallas as pl
from jax.experimental.pallas import tpu as pltpu
from jax.sharding import PartitionSpec as P

STEPS = 4
time_step = 0.5
damping = 0.1
yield_drift = 0.5
hyst_stiff = 1.0
ground_gain = 0.1
LANES = 128
HIGHEST = lax.Precision.HIGHEST
MESH = pl.DeviceIdType.MESH


def wave_kernel(
    n_gx, n_gy, capacity,
    u_prev, u_now, speeds, site_row, site_col, route_row, route_col,
    frame_disp, frame_vel, frame_acc, frame_hyst, kind_row, stiffness,
    before_out, last_out, disp_out, hyst_out, part_acc, part_vel, outgoing,
    lev_a, lev_b, spd, xsend, xrecv, ysend, yrecv,
    fd, fv, fa, fh, stiff, f_acc, f_vel, pick, placing, third, ground,
    load_sem, store_sem, xs_sem, xr_sem, ys_sem, yr_sem,
):
    ncomp, nz, cx, cy = u_now.shape
    gx = lax.axis_index("gx")
    gy = lax.axis_index("gy")
    has = (gx > 0, gx < n_gx - 1, gy > 0, gy < n_gy - 1)
    peer = ({"gx": gx - 1}, {"gx": gx + 1}, {"gy": gy - 1}, {"gy": gy + 1})

    loads = []

    def load(src, dst):
        copy = pltpu.make_async_copy(src, dst, load_sem.at[len(loads)])
        copy.start()
        loads.append(copy)
        return copy

    now_in = [load(u_now.at[c], lev_b.at[c, pl.ds(2, nz)]) for c in range(ncomp)]
    frames_in = [
        load(frame_disp, fd), load(frame_vel, fv), load(frame_acc, fa),
        load(frame_hyst, fh), load(stiffness, stiff),
    ]
    spd_in = load(speeds, spd)
    prev_in = [load(u_prev.at[c], lev_a.at[c, pl.ds(2, nz)]) for c in range(ncomp)]

    barrier = pltpu.get_barrier_semaphore()
    for d in range(4):
        @pl.when(has[d])
        def _(d=d):
            pl.semaphore_signal(barrier, inc=1, device_id=peer[d], device_id_type=MESH)

    rim = jnp.zeros((2, cx, cy), jnp.float32)
    for lev in (lev_a, lev_b):
        for c in range(ncomp):
            lev[c, pl.ds(0, 2)] = rim
            lev[c, pl.ds(nz + 2, 2)] = rim

    for side in range(2):
        @pl.when(jnp.logical_not(has[side]))
        def _(side=side):
            empty = jnp.zeros((2, nz, cy), jnp.float32)
            for k in range(STEPS):
                for c in range(ncomp):
                    xrecv[k, c, side] = empty

        @pl.when(jnp.logical_not(has[2 + side]))
        def _(side=side):
            for k in range(STEPS):
                for c in range(ncomp):
                    yrecv[k, c, side] = jnp.zeros((cx, LANES), jnp.float32)

    pl.semaphore_wait(barrier, sum(h.astype(jnp.int32) for h in has))

    def halo_copy(k, c, d):
        if d < 2:
            send, recv, ss, rs = xsend, xrecv, xs_sem, xr_sem
        else:
            send, recv, ss, rs = ysend, yrecv, ys_sem, yr_sem
        mine = d % 2
        return pltpu.make_async_remote_copy(
            src_ref=send.at[k, c, mine],
            dst_ref=recv.at[k, c, 1 - mine],
            send_sem=ss.at[k, c, mine],
            recv_sem=rs.at[k, c, 1 - mine],
            device_id=peer[d],
            device_id_type=MESH,
        )

    def send_halo(k, c):
        for d in range(4):
            @pl.when(has[d])
            def _(d=d):
                halo_copy(k, c, d).start()

    def wait_halo(k, c):
        for d in range(4):
            @pl.when(has[d])
            def _(d=d):
                recv, ss, rs = (xrecv, xs_sem, xr_sem) if d < 2 else (yrecv, ys_sem, yr_sem)
                pltpu.make_async_remote_copy(
                    src_ref=recv.at[k, c, d % 2],
                    dst_ref=recv.at[k, c, d % 2],
                    send_sem=ss.at[k, c, d % 2],
                    recv_sem=rs.at[k, c, d % 2],
                    device_id=peer[d],
                    device_id_type=MESH,
                ).wait_recv()

    def wait_sent(k, c):
        for d in range(4):
            @pl.when(has[d])
            def _(d=d):
                halo_copy(k, c, d).wait_send()

    lane = lax.broadcasted_iota(jnp.int32, (cx, LANES), 1)
    lane_plane = lane >> 1
    row = lax.broadcasted_iota(jnp.int32, (cx, cy), 0)

    def pack_edges(k, c, z, v, acc):
        head, tail = acc
        xsend[k, c, 0, 0, pl.ds(z, 1), :] = v[0:1]
        xsend[k, c, 0, 1, pl.ds(z, 1), :] = v[1:2]
        xsend[k, c, 1, 0, pl.ds(z, 1), :] = v[cx - 2:cx - 1]
        xsend[k, c, 1, 1, pl.ds(z, 1), :] = v[cx - 1:cx]
        here = lane_plane == z
        head = jnp.where(here, pltpu.roll(v[:, :LANES], 2 * z, 1), head)
        tail = jnp.where(here, pltpu.roll(v[:, cy - LANES:], 2 * z + 2, 1), tail)
        return head, tail

    blank = (jnp.zeros((cx, LANES), jnp.float32),) * 2

    def put_y(k, c, acc):
        ysend[k, c, 0] = acc[0]
        ysend[k, c, 1] = acc[1]

    def wave_step(k, c, older, newer):
        def plane(z, acc):
            u = newer[c, z + 2]
            deep = 16.0 * (newer[c, z + 1] + newer[c, z + 3]) - (newer[c, z] + newer[c, z + 4])
            xl0 = xrecv[k, c, 0, 0, pl.ds(z, 1), :]
            xl1 = xrecv[k, c, 0, 1, pl.ds(z, 1), :]
            xr0 = xrecv[k, c, 1, 0, pl.ds(z, 1), :]
            xr1 = xrecv[k, c, 1, 1, pl.ds(z, 1), :]
            w1 = jnp.where(row == 0, xl1, pltpu.roll(u, 1, 0))
            w2 = jnp.where(row == 0, xl0, jnp.where(row == 1, xl1, pltpu.roll(u, 2, 0)))
            e1 = jnp.where(row == cx - 1, xr0, pltpu.roll(u, cx - 1, 0))
            e2 = jnp.where(row == cx - 2, xr0, jnp.where(row == cx - 1, xr1, pltpu.roll(u, cx - 2, 0)))
            east = 16.0 * (w1 + e1) - (w2 + e2)
            yl = yrecv[k, c, 0]
            yr = yrecv[k, c, 1]

            def first(values, count, fix):
                return jnp.concatenate(
                    [jnp.where(lane < count, fix, values[:, :LANES]), values[:, LANES:]], axis=1
                )

            def final(values, count, fix):
                return jnp.concatenate(
                    [
                        values[:, :cy - LANES],
                        jnp.where(lane >= LANES - count, fix, values[:, cy - LANES:]),
                    ],
                    axis=1,
                )

            back = LANES - 1 - 2 * z
            s1 = first(pltpu.roll(u, 1, 1), 1, pltpu.roll(yl, back, 1))
            s2 = first(pltpu.roll(u, 2, 1), 2, pltpu.roll(yl, lax.rem(back + 1, LANES), 1))
            n1 = final(pltpu.roll(u, cy - 1, 1), 1, pltpu.roll(yr, back, 1))
            n2 = final(pltpu.roll(u, cy - 2, 1), 2, pltpu.roll(yr, back - 1, 1))
            north = 16.0 * (s1 + n1) - (s2 + n2)
            parts = [east, north, deep]
            own = parts.pop(c)
            accel = spd[0, z] * (own - 30.0 * u) + spd[1, z] * (parts[0] + parts[1] - 60.0 * u)
            v = 2.0 * u - older[c, z + 2] + accel * (1.0 / 12.0)
            older[c, z + 2] = v
            if k < STEPS - 1:
                return pack_edges(k + 1, c, z, v, acc)
            return acc

        acc = lax.fori_loop(0, nz, plane, blank)
        if k < STEPS - 1:
            put_y(k + 1, c, acc)

    for c in range(ncomp):
        now_in[c].wait()
        acc = lax.fori_loop(
            0, nz, lambda z, acc, c=c: pack_edges(0, c, z, lev_b[c, z + 2], acc), blank
        )
        put_y(0, c, acc)
        send_halo(0, c)

    for copy in frames_in:
        copy.wait()
    nf, slots = fd.shape
    wide = 2 * LANES

    def frames(i, carry):
        cols = pl.ds(pl.multiple_of(i * wide, wide), wide)
        frow = lax.broadcasted_iota(jnp.int32, (nf, wide), 0)
        d0, v0, a0 = fd[:, cols], fv[:, cols], fa[:, cols]
        change = time_step * v0 + 0.5 * time_step * time_step * a0
        nxt = d0 + change
        moved = nxt - d0
        drift = moved - jnp.where(frow < 3, 0.0, pltpu.roll(moved, 3, 0))
        hyst = jnp.clip(fh[:, cols] + drift, -yield_drift, yield_drift)
        fd[:, cols] = nxt
        fh[:, cols] = hyst
        kinds = kind_row[:, cols]
        total = (-damping) * (v0 + 0.5 * time_step * a0) - hyst_stiff * (
            hyst - jnp.where(frow >= nf - 3, 0.0, pltpu.roll(hyst, nf - 3, 0))
        )
        for kind in range(stiff.shape[0]):
            product = jnp.dot(
                stiff[kind], nxt, precision=HIGHEST, preferred_element_type=jnp.float32
            )
            total = total - jnp.where(kinds == kind, product, 0.0)
        f_acc[:, cols] = total
        f_vel[:, cols] = v0 + 0.5 * time_step * (a0 + total)
        return carry

    lax.fori_loop(0, slots // wide, frames, 0)
    stores = []

    def store(src, dst):
        copy = pltpu.make_async_copy(src, dst, store_sem.at[len(stores)])
        copy.start()
        stores.append(copy)

    store(fd, disp_out)
    store(fh, hyst_out)
    store(f_acc, part_acc)
    store(f_vel, part_vel)

    count = route_row.shape[1]
    pick[...] = (
        lax.broadcasted_iota(jnp.int32, (cy, count), 0) == site_col[...]
    ).astype(jnp.float32)
    routes = route_col[...]
    ids_i = lax.broadcasted_iota(jnp.int32, (count, count), 0)
    ids_j = lax.broadcasted_iota(jnp.int32, (count, count), 1)
    same = jnp.logical_and(routes == route_row[...], ids_j < ids_i)
    rank = jnp.sum(same.astype(jnp.float32), axis=1, keepdims=True).astype(jnp.int32)
    slot = routes * capacity + rank
    placing[...] = (
        lax.broadcasted_iota(jnp.int32, (count, slots), 1) == slot
    ).astype(jnp.float32)

    spd_in.wait()
    for copy in prev_in:
        copy.wait()

    for k in range(STEPS):
        older, newer = (lev_a, lev_b) if k % 2 == 0 else (lev_b, lev_a)
        for c in range(ncomp):
            wait_halo(k, c)
            if k == STEPS - 1:
                third[c] = older[c, 2]
            wave_step(k, c, older, newer)
            if k < STEPS - 1:
                send_halo(k + 1, c)
            if k == STEPS - 2:
                store(older.at[c, pl.ds(2, nz)], before_out.at[c])
            if k == STEPS - 1:
                store(older.at[c, pl.ds(2, nz)], last_out.at[c])
                ground[c] = ground_gain * (older[c, 2] - 2.0 * newer[c, 2] + third[c])

    cells = jnp.dot(
        ground[...].reshape(ncomp * cx, cy), pick[...],
        precision=HIGHEST, preferred_element_type=jnp.float32,
    )
    at_row = lax.broadcasted_iota(jnp.int32, (cx, count), 0) == site_row[...]
    motion = [
        jnp.sum(jnp.where(at_row, cells[c * cx:(c + 1) * cx], 0.0), axis=0, keepdims=True)
        for c in range(ncomp)
    ]
    motion = jnp.concatenate(
        motion + [jnp.zeros((8 - ncomp, count), jnp.float32)], axis=0
    )
    outgoing[...] = jnp.dot(
        motion, placing[...], precision=HIGHEST, preferred_element_type=jnp.float32
    )
    for k in range(STEPS):
        for c in range(ncomp):
            wait_sent(k, c)
    for copy in stores:
        copy.wait()


def forcing_kernel(moved_ref, acc_ref, vel_ref, acc_out, vel_out):
    nf, width = acc_ref.shape
    ids = lax.broadcasted_iota(jnp.int32, (nf, width), 0)
    phase = ids - 3 * ((ids * 43691) >> 17)
    force = jnp.where(
        phase == 0, moved_ref[0:1], jnp.where(phase == 1, moved_ref[1:2], moved_ref[2:3])
    )
    acc_out[...] = acc_ref[...] - force
    vel_out[...] = vel_ref[...] - (0.5 * time_step) * force


def shards(
    n_gx, n_gy,
    u_prev, u_now, speeds, sites, routes,
    frame_disp, frame_vel, frame_acc, frame_hyst, frame_kind, stiffness,
):
    ncomp, nz, cx, cy = u_now.shape
    devices = n_gx * n_gy
    nf, slots = frame_disp.shape
    capacity = slots // devices
    count = sites.shape[0]
    f32 = jnp.float32
    site_row = (sites // cy).reshape(1, count)
    site_col = (sites % cy).reshape(1, count)
    field = jax.ShapeDtypeStruct(u_now.shape, f32)
    frame = jax.ShapeDtypeStruct(frame_disp.shape, f32)
    anyspec = pl.BlockSpec(memory_space=pl.ANY)
    vmem = pl.BlockSpec(memory_space=pltpu.VMEM)
    level = pltpu.VMEM((ncomp, nz + 4, cx, cy), f32)
    before, last, disp, hyst, part_acc, part_vel, outgoing = pl.pallas_call(
        functools.partial(wave_kernel, n_gx, n_gy, capacity),
        out_shape=(field, field, frame, frame, frame, frame,
                   jax.ShapeDtypeStruct((8, slots), f32)),
        in_specs=[anyspec] * 3 + [vmem] * 4 + [anyspec] * 4 + [vmem, anyspec],
        out_specs=(anyspec,) * 6 + (vmem,),
        scratch_shapes=[
            level, level,
            pltpu.VMEM(speeds.shape, f32),
            pltpu.VMEM((STEPS, ncomp, 2, 2, nz, cy), f32),
            pltpu.VMEM((STEPS, ncomp, 2, 2, nz, cy), f32),
            pltpu.VMEM((STEPS, ncomp, 2, cx, LANES), f32),
            pltpu.VMEM((STEPS, ncomp, 2, cx, LANES), f32),
            pltpu.VMEM((nf, slots), f32), pltpu.VMEM((nf, slots), f32),
            pltpu.VMEM((nf, slots), f32), pltpu.VMEM((nf, slots), f32),
            pltpu.VMEM(stiffness.shape, f32),
            pltpu.VMEM((nf, slots), f32), pltpu.VMEM((nf, slots), f32),
            pltpu.VMEM((cy, count), f32),
            pltpu.VMEM((count, slots), f32),
            pltpu.VMEM((ncomp, cx, cy), f32),
            pltpu.VMEM((ncomp, cx, cy), f32),
            pltpu.SemaphoreType.DMA((2 * ncomp + 6,)),
            pltpu.SemaphoreType.DMA((2 * ncomp + 4,)),
            pltpu.SemaphoreType.DMA((STEPS, ncomp, 2)),
            pltpu.SemaphoreType.DMA((STEPS, ncomp, 2)),
            pltpu.SemaphoreType.DMA((STEPS, ncomp, 2)),
            pltpu.SemaphoreType.DMA((STEPS, ncomp, 2)),
        ],
        compiler_params=pltpu.CompilerParams(
            collective_id=0, has_side_effects=True, vmem_limit_bytes=52 * 1024 * 1024
        ),
        name="wave",
    )(
        u_prev, u_now, speeds, site_row, site_col, routes.reshape(1, count), routes,
        frame_disp, frame_vel, frame_acc, frame_hyst, frame_kind.reshape(1, slots), stiffness,
    )
    parcels = outgoing[:ncomp].reshape(ncomp, devices, capacity)
    arrived = lax.all_to_all(parcels, ("gx", "gy"), split_axis=1, concat_axis=1, tiled=True)
    moved = arrived.reshape(ncomp, slots)
    wide = min(slots, 4 * LANES)
    block = pl.BlockSpec((nf, wide), lambda i: (0, i))
    acc_next, vel_next = pl.pallas_call(
        forcing_kernel,
        grid=(slots // wide,),
        out_shape=(frame, frame),
        in_specs=[pl.BlockSpec((ncomp, wide), lambda i: (0, i)), block, block],
        out_specs=(block, block),
        name="forcing",
    )(moved, part_acc, part_vel)
    return before, last, disp, vel_next, acc_next, hyst


def solution(mesh):
    cells = P(None, None, "gx", "gy")
    both = ("gx", "gy")
    frame = P(None, both)
    return jax.shard_map(
        functools.partial(shards, mesh.shape["gx"], mesh.shape["gy"]),
        mesh=mesh,
        in_specs=(cells, cells, cells, P(both), P(both, None), frame, frame, frame, frame,
                  P(both), P()),
        out_specs=(cells, cells, frame, frame, frame, frame),
        check_vma=False,
    )
```

```python
import functools

import jax
import jax.numpy as jnp
from jax import lax
from jax.experimental import pallas as pl
from jax.experimental.pallas import tpu as pltpu
from jax.sharding import PartitionSpec as P

STEPS = 4
time_step = 0.5
damping = 0.1
yield_drift = 0.5
hyst_stiff = 1.0
ground_gain = 0.1
LANES = 128
HIGHEST = lax.Precision.HIGHEST
MESH = pl.DeviceIdType.MESH


def lines(n_gx, n_gy):
    return (("gy", n_gy), ("gx", n_gx))


def wave_kernel(
    n_gx, n_gy, capacity,
    u_prev, u_now, speeds, sites, routes,
    frame_disp, frame_vel, frame_acc, frame_hyst, frame_kind, stiffness,
    before_out, last_out, disp_out, vel_out, acc_out, hyst_out,
    lev_a, lev_b, spd, xsend, xrecv, ysend, yrecv,
    fd, fv, fa, fh, stiff, f_acc, f_vel, site_row, route_row, kind_row,
    pick, placing, third, ground, send_1, recv_1, send_2, recv_2, moved,
    load_sem, store_sem, xs_sem, xr_sem, ys_sem, yr_sem,
    send_1_sem, recv_1_sem, send_2_sem, recv_2_sem,
):
    ncomp, nz, cx, cy = u_now.shape
    tiles = cy // LANES
    place = {"gx": lax.axis_index("gx"), "gy": lax.axis_index("gy")}
    gx, gy = place["gx"], place["gy"]
    has = (gx > 0, gx < n_gx - 1, gy > 0, gy < n_gy - 1)
    peer = ({"gx": gx - 1}, {"gx": gx + 1}, {"gy": gy - 1}, {"gy": gy + 1})

    loads = []

    def load(src, dst):
        copy = pltpu.make_async_copy(src, dst, load_sem.at[len(loads)])
        copy.start()
        loads.append(copy)
        return copy

    now_in = [load(u_now.at[c], lev_b.at[c, pl.ds(2, nz)]) for c in range(ncomp)]
    field_in = [load(speeds, spd)] + [
        load(u_prev.at[c], lev_a.at[c, pl.ds(2, nz)]) for c in range(ncomp)
    ]
    frames_in = [
        load(frame_disp, fd), load(frame_vel, fv), load(frame_acc, fa),
        load(frame_hyst, fh), load(stiffness, stiff),
        load(frame_kind, kind_row), load(sites, site_row), load(routes, route_row),
    ]

    barrier = pltpu.get_barrier_semaphore()
    for axis, size in lines(n_gx, n_gy):
        for off in range(1, size):
            pl.semaphore_signal(
                barrier, inc=1, device_id={axis: lax.rem(place[axis] + off, size)},
                device_id_type=MESH,
            )

    rim = jnp.zeros((2, cx, cy), jnp.float32)
    for lev in (lev_a, lev_b):
        for c in range(ncomp):
            lev[c, pl.ds(0, 2)] = rim
            lev[c, pl.ds(nz + 2, 2)] = rim

    for side in range(2):
        @pl.when(jnp.logical_not(has[side]))
        def _(side=side):
            empty = jnp.zeros(xrecv.shape[3:], jnp.float32)
            for k in range(STEPS):
                for c in range(ncomp):
                    xrecv[k, c, side] = empty

        @pl.when(jnp.logical_not(has[2 + side]))
        def _(side=side):
            for k in range(STEPS):
                for c in range(ncomp):
                    for t in range(2):
                        yrecv[k, c, t, side] = jnp.zeros((cx, LANES), jnp.float32)

    pl.semaphore_wait(barrier, n_gx + n_gy - 2)

    def planes(k, t):
        cut = 2 * (STEPS - k) - 1
        return (0, cut) if t == 0 else (cut, nz)

    def halo_copy(k, c, t, d):
        mine = d % 2
        if d < 2:
            low, high = planes(k, t)
            zs = pl.ds(low, high - low)
            src, dst = xsend.at[k, c, mine, zs], xrecv.at[k, c, 1 - mine, zs]
            ss, rs = xs_sem, xr_sem
        else:
            src, dst = ysend.at[k, c, t, mine], yrecv.at[k, c, t, 1 - mine]
            ss, rs = ys_sem, yr_sem
        return pltpu.make_async_remote_copy(
            src_ref=src, dst_ref=dst,
            send_sem=ss.at[k, c, t, mine], recv_sem=rs.at[k, c, t, 1 - mine],
            device_id=peer[d], device_id_type=MESH,
        )

    def send_halo(k, c, t):
        for d in range(4):
            @pl.when(has[d])
            def _(d=d):
                halo_copy(k, c, t, d).start()

    def wait_halo(k, c, t):
        low, high = planes(k, t)
        zs = pl.ds(low, high - low)
        for d in range(4):
            @pl.when(has[d])
            def _(d=d):
                if d < 2:
                    slot, ss, rs = xrecv.at[k, c, d % 2, zs], xs_sem, xr_sem
                else:
                    slot, ss, rs = yrecv.at[k, c, t, d % 2], ys_sem, yr_sem
                pltpu.make_async_remote_copy(
                    src_ref=slot, dst_ref=slot,
                    send_sem=ss.at[k, c, t, d % 2], recv_sem=rs.at[k, c, t, d % 2],
                    device_id=peer[d], device_id_type=MESH,
                ).wait_recv()

    def wait_sent(k, c, t):
        for d in range(4):
            @pl.when(has[d])
            def _(d=d):
                halo_copy(k, c, t, d).wait_send()

    lane = lax.broadcasted_iota(jnp.int32, (cx, LANES), 1)
    lane_plane = lane >> 1
    row = lax.broadcasted_iota(jnp.int32, (cx, cy), 0)

    def pack_edges(k, c, z, v, acc):
        head, tail = acc
        for side in range(2):
            for r in range(2):
                at = r if side == 0 else cx - 2 + r
                for t in range(tiles):
                    xsend[k, c, side, z, pl.ds(r * tiles + t, 1), :] = (
                        v[at:at + 1, t * LANES:(t + 1) * LANES]
                    )
        here = lane_plane == z
        head = jnp.where(here, pltpu.roll(v[:, :LANES], 2 * z, 1), head)
        tail = jnp.where(here, pltpu.roll(v[:, cy - LANES:], lax.rem(2 * z + 2, LANES), 1), tail)
        return head, tail

    blank = (jnp.zeros((cx, LANES), jnp.float32),) * 2

    def put_y(k, c, t, acc):
        ysend[k, c, t, 0] = acc[0]
        ysend[k, c, t, 1] = acc[1]

    def wave_part(k, c, low, high, t, older, newer, acc):
        def plane(z, acc):
            u = newer[c, z + 2]
            deep = 16.0 * (newer[c, z + 1] + newer[c, z + 3]) - (newer[c, z] + newer[c, z + 4])

            def edge(side, r):
                return jnp.concatenate(
                    [xrecv[k, c, side, z, pl.ds(r * tiles + i, 1), :] for i in range(tiles)],
                    axis=1,
                )

            xl0, xl1, xr0, xr1 = edge(0, 0), edge(0, 1), edge(1, 0), edge(1, 1)
            w1 = jnp.where(row == 0, xl1, pltpu.roll(u, 1, 0))
            w2 = jnp.where(row == 0, xl0, jnp.where(row == 1, xl1, pltpu.roll(u, 2, 0)))
            e1 = jnp.where(row == cx - 1, xr0, pltpu.roll(u, cx - 1, 0))
            e2 = jnp.where(row == cx - 2, xr0, jnp.where(row == cx - 1, xr1, pltpu.roll(u, cx - 2, 0)))
            east = 16.0 * (w1 + e1) - (w2 + e2)
            yl = yrecv[k, c, t, 0]
            yr = yrecv[k, c, t, 1]

            def first(values, count, fix):
                return jnp.concatenate(
                    [jnp.where(lane < count, fix, values[:, :LANES]), values[:, LANES:]], axis=1
                )

            def final(values, count, fix):
                return jnp.concatenate(
                    [
                        values[:, :cy - LANES],
                        jnp.where(lane >= LANES - count, fix, values[:, cy - LANES:]),
                    ],
                    axis=1,
                )

            back = LANES - 1 - 2 * z
            s1 = first(pltpu.roll(u, 1, 1), 1, pltpu.roll(yl, back, 1))
            s2 = first(pltpu.roll(u, 2, 1), 2, pltpu.roll(yl, lax.rem(back + 1, LANES), 1))
            n1 = final(pltpu.roll(u, cy - 1, 1), 1, pltpu.roll(yr, back, 1))
            n2 = final(pltpu.roll(u, cy - 2, 1), 2, pltpu.roll(yr, back - 1, 1))
            north = 16.0 * (s1 + n1) - (s2 + n2)
            parts = [east, north, deep]
            own = parts.pop(c)
            accel = spd[0, z] * (own - 30.0 * u) + spd[1, z] * (parts[0] + parts[1] - 60.0 * u)
            v = 2.0 * u - older[c, z + 2] + accel * (1.0 / 12.0)
            older[c, z + 2] = v
            if k < STEPS - 1:
                return pack_edges(k + 1, c, z, v, acc)
            return acc

        return lax.fori_loop(low, high, plane, acc)

    def levels(k):
        return (lev_a, lev_b) if k % 2 == 0 else (lev_b, lev_a)

    def top_step(k):
        older, newer = levels(k)
        low, high = planes(k, 0)
        for c in range(ncomp):
            wait_halo(k, c, 0)
            if k == STEPS - 1:
                third[c] = older[c, 2]
                wave_part(k, c, low, high, 0, older, newer, blank)
                ground[c] = ground_gain * (older[c, 2] - 2.0 * newer[c, 2] + third[c])
            else:
                cut = planes(k + 1, 0)[1]
                acc = wave_part(k, c, low, cut, 0, older, newer, blank)
                put_y(k + 1, c, 0, acc)
                send_halo(k + 1, c, 0)
                acc = wave_part(k, c, cut, high, 0, older, newer, blank)
                put_y(k + 1, c, 1, acc)

    def deep_step(k, c):
        older, newer = levels(k)
        low, high = planes(k, 1)
        wait_halo(k, c, 1)
        if k < STEPS - 1:
            acc = (ysend[k + 1, c, 1, 0], ysend[k + 1, c, 1, 1])
            acc = wave_part(k, c, low, high, 1, older, newer, acc)
            put_y(k + 1, c, 1, acc)
            send_halo(k + 1, c, 1)
        else:
            wave_part(k, c, low, high, 1, older, newer, blank)

    def first_edges(c, t):
        low, high = planes(0, t)
        acc = lax.fori_loop(
            low, high, lambda z, acc: pack_edges(0, c, z, lev_b[c, z + 2], acc), blank
        )
        put_y(0, c, t, acc)
        send_halo(0, c, t)

    stores = []

    def store(src, dst):
        copy = pltpu.make_async_copy(src, dst, store_sem.at[len(stores)])
        copy.start()
        stores.append(copy)

    nf, slots = fd.shape
    wide = 2 * LANES

    def frames(i, carry):
        cols = pl.ds(pl.multiple_of(i * wide, wide), wide)
        frow = lax.broadcasted_iota(jnp.int32, (nf, wide), 0)
        d0, v0, a0 = fd[:, cols], fv[:, cols], fa[:, cols]
        change = time_step * v0 + 0.5 * time_step * time_step * a0
        nxt = d0 + change
        moving = nxt - d0
        drift = moving - jnp.where(frow < 3, 0.0, pltpu.roll(moving, 3, 0))
        hyst = jnp.clip(fh[:, cols] + drift, -yield_drift, yield_drift)
        fd[:, cols] = nxt
        fh[:, cols] = hyst
        kinds = kind_row[:, cols]
        total = (-damping) * (v0 + 0.5 * time_step * a0) - hyst_stiff * (
            hyst - jnp.where(frow >= nf - 3, 0.0, pltpu.roll(hyst, nf - 3, 0))
        )
        for kind in range(stiff.shape[0]):
            product = jnp.dot(
                stiff[kind], nxt, precision=HIGHEST, preferred_element_type=jnp.float32
            )
            total = total - jnp.where(kinds == kind, product, 0.0)
        f_acc[:, cols] = total
        f_vel[:, cols] = v0 + 0.5 * time_step * (a0 + total)
        return carry

    def locate():
        count = route_row.shape[1]
        route = route_row[...]
        pick[...] = (
            lax.broadcasted_iota(jnp.int32, (cy, count), 0) == (site_row[...] & (cy - 1))
        ).astype(jnp.float32)
        named = (
            lax.broadcasted_iota(jnp.int32, (n_gx * n_gy, count), 0) == route
        ).astype(jnp.float32)
        earlier = (
            lax.broadcasted_iota(jnp.int32, (count, count), 0)
            < lax.broadcasted_iota(jnp.int32, (count, count), 1)
        ).astype(jnp.float32)
        ahead = jnp.dot(named, earlier, precision=HIGHEST, preferred_element_type=jnp.float32)
        rank = jnp.sum(ahead * named, axis=0, keepdims=True).astype(jnp.int32)
        owner_x = route >> (n_gy.bit_length() - 1)
        owner_y = route & (n_gy - 1)
        spot = owner_y * (n_gx * capacity) + owner_x * capacity + rank
        placing[...] = (
            lax.broadcasted_iota(jnp.int32, (slots, count), 0) == spot
        ).astype(jnp.float32)

    def parcel(axis, size, send, recv, ss, rs, off, sending):
        me = place[axis]
        to = lax.rem(me + off, size)
        source = lax.rem(me + size - off, size)
        return pltpu.make_async_remote_copy(
            src_ref=send.at[to],
            dst_ref=recv.at[me if sending else source],
            send_sem=ss.at[off], recv_sem=rs.at[off],
            device_id={axis: to}, device_id_type=MESH,
        )

    hop_1 = ("gy", n_gy, send_1, recv_1, send_1_sem, recv_1_sem)
    hop_2 = ("gx", n_gx, send_2, recv_2, send_2_sem, recv_2_sem)

    def start_hop(hop):
        axis, size, send, recv = hop[:4]
        for off in range(1, size):
            parcel(*hop, off, True).start()
        recv[place[axis]] = send[place[axis]]

    def end_hop(hop):
        for off in range(1, hop[1]):
            parcel(*hop, off, False).wait_recv()

    def post_motion():
        count = route_row.shape[1]
        cells = jnp.dot(
            ground[...].reshape(ncomp * cx, cy), pick[...],
            precision=HIGHEST, preferred_element_type=jnp.float32,
        )
        at_row = lax.broadcasted_iota(jnp.int32, (cx, count), 0) == (
            site_row[...] >> (cy.bit_length() - 1)
        )
        motion = jnp.concatenate(
            [
                jnp.sum(jnp.where(at_row, cells[c * cx:(c + 1) * cx], 0.0), axis=0, keepdims=True)
                for c in range(ncomp)
            ]
            + [jnp.zeros((8 - ncomp, count), jnp.float32)],
            axis=0,
        )
        outgoing = lax.dot_general(
            motion, placing[...], (((1,), (1,)), ((), ())),
            precision=HIGHEST, preferred_element_type=jnp.float32,
        )
        width = n_gx * capacity
        for y in range(n_gy):
            send_1[y] = outgoing[:, y * width:(y + 1) * width]
        start_hop(hop_1)

    part = n_gy * capacity
    narrow = lax.broadcasted_iota(jnp.int32, (8, LANES), 1)

    def relay_motion():
        end_hop(hop_1)
        for x in range(n_gx):
            tile, start = divmod(x * capacity, LANES)
            total = jnp.zeros((8, LANES), jnp.float32)
            for y in range(n_gy):
                piece = recv_1[y, :, tile * LANES:(tile + 1) * LANES]
                shift = (y * capacity - start) % LANES
                if shift:
                    piece = pltpu.roll(piece, shift, 1)
                here = jnp.logical_and(narrow >= y * capacity, narrow < (y + 1) * capacity)
                total = jnp.where(here, piece, total)
            send_2[x] = total
        start_hop(hop_2)

    def add_forcing():
        end_hop(hop_2)
        per_tile = LANES // part
        for tile in range(slots // LANES):
            total = recv_2[tile * per_tile]
            for i in range(1, per_tile):
                piece = pltpu.roll(recv_2[tile * per_tile + i], i * part, 1)
                total = jnp.where(narrow >= i * part, piece, total)
            moved[:, tile * LANES:(tile + 1) * LANES] = total

        def chunk(i, carry):
            cols = pl.ds(pl.multiple_of(i * LANES, LANES), LANES)
            ids = lax.broadcasted_iota(jnp.int32, (nf, LANES), 0)
            phase = ids - 3 * ((ids * 43691) >> 17)
            m = moved[:, cols]
            force = jnp.where(phase == 0, m[0:1], jnp.where(phase == 1, m[1:2], m[2:3]))
            f_acc[:, cols] = f_acc[:, cols] - force
            f_vel[:, cols] = f_vel[:, cols] - (0.5 * time_step) * force
            return carry

        lax.fori_loop(0, slots // LANES, chunk, 0)
        store(f_acc, acc_out)
        store(f_vel, vel_out)

    for c in range(ncomp):
        now_in[c].wait()
        first_edges(c, 0)
    for c in range(ncomp):
        first_edges(c, 1)
    for copy in field_in:
        copy.wait()
    top_step(0)
    for copy in frames_in:
        copy.wait()
    lax.fori_loop(0, slots // wide, frames, 0)
    store(fd, disp_out)
    store(fh, hyst_out)
    top_step(1)
    locate()
    deep_step(0, 0)
    top_step(2)
    deep_step(0, 1)
    top_step(3)
    post_motion()
    deep_step(0, 2)
    deep_step(1, 0)
    relay_motion()
    deep_step(1, 1)
    deep_step(1, 2)
    deep_step(2, 0)
    store(lev_a.at[0, pl.ds(2, nz)], before_out.at[0])
    add_forcing()
    for c in range(1, ncomp):
        deep_step(2, c)
        store(lev_a.at[c, pl.ds(2, nz)], before_out.at[c])
    for c in range(ncomp):
        deep_step(3, c)
        store(lev_b.at[c, pl.ds(2, nz)], last_out.at[c])
    for k in range(STEPS):
        for c in range(ncomp):
            for t in range(2):
                wait_sent(k, c, t)
    for hop in (hop_1, hop_2):
        for off in range(1, hop[1]):
            parcel(*hop, off, True).wait_send()
    for copy in stores:
        copy.wait()


def shards(
    n_gx, n_gy,
    u_prev, u_now, speeds, sites, routes,
    frame_disp, frame_vel, frame_acc, frame_hyst, frame_kind, stiffness,
):
    ncomp, nz, cx, cy = u_now.shape
    devices = n_gx * n_gy
    nf, slots = frame_disp.shape
    capacity = slots // devices
    count = sites.shape[0]
    f32 = jnp.float32
    i32 = jnp.int32
    field = jax.ShapeDtypeStruct(u_now.shape, f32)
    frame = jax.ShapeDtypeStruct(frame_disp.shape, f32)
    anyspec = pl.BlockSpec(memory_space=pl.ANY)
    level = pltpu.VMEM((ncomp, nz + 4, cx, cy), f32)
    x_edges = pltpu.VMEM((STEPS, ncomp, 2, nz, 2 * cy // LANES, LANES), f32)
    y_edges = pltpu.VMEM((STEPS, ncomp, 2, 2, cx, LANES), f32)
    batch = pltpu.VMEM((nf, slots), f32)
    plane = pltpu.VMEM((ncomp, cx, cy), f32)
    first_hop = pltpu.VMEM((n_gy, 8, n_gx * capacity), f32)
    second_hop = pltpu.VMEM((n_gx, 8, LANES), f32)
    halo_sem = pltpu.SemaphoreType.DMA((STEPS, ncomp, 2, 2))
    return pl.pallas_call(
        functools.partial(wave_kernel, n_gx, n_gy, capacity),
        out_shape=(field, field, frame, frame, frame, frame),
        in_specs=[anyspec] * 11,
        out_specs=(anyspec,) * 6,
        scratch_shapes=[
            level, level, pltpu.VMEM(speeds.shape, f32),
            x_edges, x_edges, y_edges, y_edges,
            batch, batch, batch, batch, pltpu.VMEM(stiffness.shape, f32), batch, batch,
            pltpu.VMEM((1, count), i32), pltpu.VMEM((1, count), i32), pltpu.VMEM((1, slots), i32),
            pltpu.VMEM((cy, count), f32), pltpu.VMEM((slots, count), f32),
            plane, plane, first_hop, first_hop, second_hop, second_hop,
            pltpu.VMEM((8, slots), f32),
            pltpu.SemaphoreType.DMA((2 * ncomp + 9,)),
            pltpu.SemaphoreType.DMA((2 * ncomp + 4,)),
            halo_sem, halo_sem, halo_sem, halo_sem,
            pltpu.SemaphoreType.DMA((n_gy,)), pltpu.SemaphoreType.DMA((n_gy,)),
            pltpu.SemaphoreType.DMA((n_gx,)), pltpu.SemaphoreType.DMA((n_gx,)),
        ],
        compiler_params=pltpu.CompilerParams(
            collective_id=0, has_side_effects=True, vmem_limit_bytes=52 * 1024 * 1024
        ),
        name="wave",
    )(
        u_prev, u_now, speeds, sites.reshape(1, count), routes.reshape(1, count),
        frame_disp, frame_vel, frame_acc, frame_hyst, frame_kind.reshape(1, slots), stiffness,
    )


def solution(mesh):
    cells = P(None, None, "gx", "gy")
    both = ("gx", "gy")
    frame = P(None, both)
    return jax.shard_map(
        functools.partial(shards, mesh.shape["gx"], mesh.shape["gy"]),
        mesh=mesh,
        in_specs=(cells, cells, cells, P(both), P(both, None), frame, frame, frame, frame,
                  P(both), P()),
        out_specs=(cells, cells, frame, frame, frame, frame),
        check_vma=False,
    )
```

```python
import functools

import jax
import jax.numpy as jnp
from jax import lax
from jax.experimental import pallas as pl
from jax.experimental.pallas import tpu as pltpu
from jax.sharding import PartitionSpec as P

STEPS = 4
time_step = 0.5
damping = 0.1
yield_drift = 0.5
hyst_stiff = 1.0
ground_gain = 0.1
LANES = 128
GROUP = 2
HIGHEST = lax.Precision.HIGHEST
MESH = pl.DeviceIdType.MESH


def lines(n_gx, n_gy):
    return (("gy", n_gy), ("gx", n_gx))


def wave_kernel(
    n_gx, n_gy, capacity,
    u_prev, u_now, speeds, sites, routes,
    frame_disp, frame_vel, frame_acc, frame_hyst, frame_kind, stiffness,
    before_out, last_out, disp_out, vel_out, acc_out, hyst_out,
    lev_a, lev_b, spd, xsend, xrecv, ysend, yrecv,
    fd, fv, fa, fh, stiff, f_acc, f_vel, site_row, route_row, kind_row,
    pick, placing, third, ground, send_1, recv_1, send_2, recv_2, moved,
    load_sem, store_sem, xs_sem, xr_sem, ys_sem, yr_sem,
    send_1_sem, recv_1_sem, send_2_sem, recv_2_sem,
):
    ncomp, nz, cx, cy = u_now.shape
    tiles = cy // LANES
    place = {"gx": lax.axis_index("gx"), "gy": lax.axis_index("gy")}
    gx, gy = place["gx"], place["gy"]
    has = (gx > 0, gx < n_gx - 1, gy > 0, gy < n_gy - 1)
    peer = ({"gx": gx - 1}, {"gx": gx + 1}, {"gy": gy - 1}, {"gy": gy + 1})

    loads = []

    def load(src, dst):
        copy = pltpu.make_async_copy(src, dst, load_sem.at[len(loads)])
        copy.start()
        loads.append(copy)
        return copy

    now_in = [load(u_now.at[c], lev_b.at[c, pl.ds(2, nz)]) for c in range(ncomp)]
    field_in = [load(speeds, spd)] + [
        load(u_prev.at[c], lev_a.at[c, pl.ds(2, nz)]) for c in range(ncomp)
    ]
    frames_in = [
        load(frame_disp, fd), load(frame_vel, fv), load(frame_acc, fa),
        load(frame_hyst, fh), load(stiffness, stiff),
        load(frame_kind, kind_row), load(sites, site_row), load(routes, route_row),
    ]

    barrier = pltpu.get_barrier_semaphore()
    for axis, size in lines(n_gx, n_gy):
        for off in range(1, size):
            pl.semaphore_signal(
                barrier, inc=1, device_id={axis: lax.rem(place[axis] + off, size)},
                device_id_type=MESH,
            )

    rim = jnp.zeros((2, cx, cy), jnp.float32)
    for lev in (lev_a, lev_b):
        for c in range(ncomp):
            lev[c, pl.ds(0, 2)] = rim
            lev[c, pl.ds(nz + 2, 2)] = rim

    for side in range(2):
        @pl.when(jnp.logical_not(has[side]))
        def _(side=side):
            empty = jnp.zeros(xrecv.shape[3:], jnp.float32)
            for k in range(STEPS):
                for c in range(ncomp):
                    xrecv[k, c, side] = empty

        @pl.when(jnp.logical_not(has[2 + side]))
        def _(side=side):
            for k in range(STEPS):
                for c in range(ncomp):
                    for t in range(2):
                        yrecv[k, c, t, side] = jnp.zeros((cx, LANES), jnp.float32)

    pl.semaphore_wait(barrier, n_gx + n_gy - 2)

    def planes(k, t):
        cut = 2 * (STEPS - k) - 1
        return (0, cut) if t == 0 else (cut, nz)

    def halo_copy(k, c, t, d):
        mine = d % 2
        if d < 2:
            low, high = planes(k, t)
            zs = pl.ds(low, high - low)
            src, dst = xsend.at[k, c, mine, zs], xrecv.at[k, c, 1 - mine, zs]
            ss, rs = xs_sem, xr_sem
        else:
            src, dst = ysend.at[k, c, t, mine], yrecv.at[k, c, t, 1 - mine]
            ss, rs = ys_sem, yr_sem
        return pltpu.make_async_remote_copy(
            src_ref=src, dst_ref=dst,
            send_sem=ss.at[k, c, t, mine], recv_sem=rs.at[k, c, t, 1 - mine],
            device_id=peer[d], device_id_type=MESH,
        )

    def send_halo(k, c, t):
        for d in range(4):
            @pl.when(has[d])
            def _(d=d):
                halo_copy(k, c, t, d).start()

    def wait_halo(k, c, t):
        low, high = planes(k, t)
        zs = pl.ds(low, high - low)
        for d in range(4):
            @pl.when(has[d])
            def _(d=d):
                if d < 2:
                    slot, ss, rs = xrecv.at[k, c, d % 2, zs], xs_sem, xr_sem
                else:
                    slot, ss, rs = yrecv.at[k, c, t, d % 2], ys_sem, yr_sem
                pltpu.make_async_remote_copy(
                    src_ref=slot, dst_ref=slot,
                    send_sem=ss.at[k, c, t, d % 2], recv_sem=rs.at[k, c, t, d % 2],
                    device_id=peer[d], device_id_type=MESH,
                ).wait_recv()

    def wait_sent(k, c, t):
        for d in range(4):
            @pl.when(has[d])
            def _(d=d):
                halo_copy(k, c, t, d).wait_send()

    lane = lax.broadcasted_iota(jnp.int32, (cx, LANES), 1)
    lane_plane = lane >> 1
    row = lax.broadcasted_iota(jnp.int32, (8, cy), 0)

    def each_plane(low, high, body, acc):
        whole = (high - low) // GROUP

        def group(i, acc):
            for j in range(GROUP):
                acc = body(low + i * GROUP + j, acc)
            return acc

        if whole:
            acc = lax.fori_loop(0, whole, group, acc)
        for z in range(low + whole * GROUP, high):
            acc = body(z, acc)
        return acc

    def pack_edges(k, c, z, v, acc):
        head, tail = acc
        for side in range(2):
            for r in range(2):
                at = r if side == 0 else cx - 2 + r
                for t in range(tiles):
                    xsend[k, c, side, z, pl.ds(r * tiles + t, 1), :] = (
                        v[at:at + 1, t * LANES:(t + 1) * LANES]
                    )
        here = lane_plane == z
        head = jnp.where(here, pltpu.roll(v[:, :LANES], 2 * z, 1), head)
        tail = jnp.where(here, pltpu.roll(v[:, cy - LANES:], (2 * z + 2) % LANES, 1), tail)
        return head, tail

    blank = (jnp.zeros((cx, LANES), jnp.float32),) * 2

    def put_y(k, c, t, acc):
        ysend[k, c, t, 0] = acc[0]
        ysend[k, c, t, 1] = acc[1]

    def wave_part(k, c, low, high, t, older, newer, acc):
        def plane(z, acc):
            u = newer[c, z + 2]
            deep = 16.0 * (newer[c, z + 1] + newer[c, z + 3]) - (newer[c, z] + newer[c, z + 4])

            def edge(side, r):
                return jnp.concatenate(
                    [xrecv[k, c, side, z, pl.ds(r * tiles + i, 1), :] for i in range(tiles)],
                    axis=1,
                )

            xl0, xl1, xr0, xr1 = edge(0, 0), edge(0, 1), edge(1, 0), edge(1, 1)
            def upper(values, *fixes):
                rim = values[:8]
                for at, fix in fixes:
                    rim = jnp.where(row == at, fix, rim)
                return jnp.concatenate([rim, values[8:]], axis=0)

            def lower(values, *fixes):
                rim = values[cx - 8:]
                for at, fix in fixes:
                    rim = jnp.where(row == at, fix, rim)
                return jnp.concatenate([values[:cx - 8], rim], axis=0)

            w1 = upper(pltpu.roll(u, 1, 0), (0, xl1))
            w2 = upper(pltpu.roll(u, 2, 0), (0, xl0), (1, xl1))
            e1 = lower(pltpu.roll(u, cx - 1, 0), (7, xr0))
            e2 = lower(pltpu.roll(u, cx - 2, 0), (6, xr0), (7, xr1))
            east = 16.0 * (w1 + e1) - (w2 + e2)
            yl = yrecv[k, c, t, 0]
            yr = yrecv[k, c, t, 1]

            def first(values, count, fix):
                return jnp.concatenate(
                    [jnp.where(lane < count, fix, values[:, :LANES]), values[:, LANES:]], axis=1
                )

            def final(values, count, fix):
                return jnp.concatenate(
                    [
                        values[:, :cy - LANES],
                        jnp.where(lane >= LANES - count, fix, values[:, cy - LANES:]),
                    ],
                    axis=1,
                )

            back = LANES - 1 - 2 * z
            s1 = first(pltpu.roll(u, 1, 1), 1, pltpu.roll(yl, back, 1))
            s2 = first(pltpu.roll(u, 2, 1), 2, pltpu.roll(yl, (back + 1) % LANES, 1))
            n1 = final(pltpu.roll(u, cy - 1, 1), 1, pltpu.roll(yr, back, 1))
            n2 = final(pltpu.roll(u, cy - 2, 1), 2, pltpu.roll(yr, back - 1, 1))
            north = 16.0 * (s1 + n1) - (s2 + n2)
            parts = [east, north, deep]
            own = parts.pop(c)
            accel = spd[0, z] * (own - 30.0 * u) + spd[1, z] * (parts[0] + parts[1] - 60.0 * u)
            v = 2.0 * u - older[c, z + 2] + accel * (1.0 / 12.0)
            older[c, z + 2] = v
            if k < STEPS - 1:
                return pack_edges(k + 1, c, z, v, acc)
            return acc

        return each_plane(low, high, plane, acc)

    def levels(k):
        return (lev_a, lev_b) if k % 2 == 0 else (lev_b, lev_a)

    def top_step(k):
        older, newer = levels(k)
        low, high = planes(k, 0)
        for c in range(ncomp):
            wait_halo(k, c, 0)
            if k == STEPS - 1:
                third[c] = older[c, 2]
                wave_part(k, c, low, high, 0, older, newer, blank)
                ground[c] = ground_gain * (older[c, 2] - 2.0 * newer[c, 2] + third[c])
            else:
                cut = planes(k + 1, 0)[1]
                acc = wave_part(k, c, low, cut, 0, older, newer, blank)
                put_y(k + 1, c, 0, acc)
                send_halo(k + 1, c, 0)
                acc = wave_part(k, c, cut, high, 0, older, newer, blank)
                put_y(k + 1, c, 1, acc)

    def deep_step(k, c):
        older, newer = levels(k)
        low, high = planes(k, 1)
        wait_halo(k, c, 1)
        if k < STEPS - 1:
            acc = (ysend[k + 1, c, 1, 0], ysend[k + 1, c, 1, 1])
            acc = wave_part(k, c, low, high, 1, older, newer, acc)
            put_y(k + 1, c, 1, acc)
            send_halo(k + 1, c, 1)
        else:
            wave_part(k, c, low, high, 1, older, newer, blank)

    def first_edges(c, t):
        low, high = planes(0, t)
        acc = each_plane(
            low, high, lambda z, acc: pack_edges(0, c, z, lev_b[c, z + 2], acc), blank
        )
        put_y(0, c, t, acc)
        send_halo(0, c, t)

    stores = []

    def store(src, dst):
        copy = pltpu.make_async_copy(src, dst, store_sem.at[len(stores)])
        copy.start()
        stores.append(copy)

    nf, slots = fd.shape
    wide = 2 * LANES

    def frames(i, carry):
        cols = pl.ds(pl.multiple_of(i * wide, wide), wide)
        frow = lax.broadcasted_iota(jnp.int32, (nf, wide), 0)
        d0, v0, a0 = fd[:, cols], fv[:, cols], fa[:, cols]
        change = time_step * v0 + 0.5 * time_step * time_step * a0
        nxt = d0 + change
        moving = nxt - d0
        drift = moving - jnp.where(frow < 3, 0.0, pltpu.roll(moving, 3, 0))
        hyst = jnp.clip(fh[:, cols] + drift, -yield_drift, yield_drift)
        fd[:, cols] = nxt
        fh[:, cols] = hyst
        kinds = kind_row[:, cols]
        total = (-damping) * (v0 + 0.5 * time_step * a0) - hyst_stiff * (
            hyst - jnp.where(frow >= nf - 3, 0.0, pltpu.roll(hyst, nf - 3, 0))
        )
        for kind in range(stiff.shape[0]):
            product = jnp.dot(
                stiff[kind], nxt, precision=HIGHEST, preferred_element_type=jnp.float32
            )
            total = total - jnp.where(kinds == kind, product, 0.0)
        f_acc[:, cols] = total
        f_vel[:, cols] = v0 + 0.5 * time_step * (a0 + total)
        return carry

    def locate():
        count = route_row.shape[1]
        route = route_row[...]
        pick[...] = (
            lax.broadcasted_iota(jnp.int32, (cy, count), 0) == (site_row[...] & (cy - 1))
        ).astype(jnp.float32)
        named = (
            lax.broadcasted_iota(jnp.int32, (n_gx * n_gy, count), 0) == route
        ).astype(jnp.float32)
        earlier = (
            lax.broadcasted_iota(jnp.int32, (count, count), 0)
            < lax.broadcasted_iota(jnp.int32, (count, count), 1)
        ).astype(jnp.float32)
        ahead = jnp.dot(named, earlier, precision=HIGHEST, preferred_element_type=jnp.float32)
        rank = jnp.sum(ahead * named, axis=0, keepdims=True).astype(jnp.int32)
        owner_x = route >> (n_gy.bit_length() - 1)
        owner_y = route & (n_gy - 1)
        spot = owner_y * (n_gx * capacity) + owner_x * capacity + rank
        placing[...] = (
            lax.broadcasted_iota(jnp.int32, (slots, count), 0) == spot
        ).astype(jnp.float32)

    def parcel(axis, size, send, recv, ss, rs, off, sending):
        me = place[axis]
        to = lax.rem(me + off, size)
        source = lax.rem(me + size - off, size)
        return pltpu.make_async_remote_copy(
            src_ref=send.at[to],
            dst_ref=recv.at[me if sending else source],
            send_sem=ss.at[off], recv_sem=rs.at[off],
            device_id={axis: to}, device_id_type=MESH,
        )

    hop_1 = ("gy", n_gy, send_1, recv_1, send_1_sem, recv_1_sem)
    hop_2 = ("gx", n_gx, send_2, recv_2, send_2_sem, recv_2_sem)

    def start_hop(hop):
        axis, size, send, recv = hop[:4]
        for off in range(1, size):
            parcel(*hop, off, True).start()
        recv[place[axis]] = send[place[axis]]

    def end_hop(hop):
        for off in range(1, hop[1]):
            parcel(*hop, off, False).wait_recv()

    def post_motion():
        count = route_row.shape[1]
        cells = jnp.dot(
            ground[...].reshape(ncomp * cx, cy), pick[...],
            precision=HIGHEST, preferred_element_type=jnp.float32,
        )
        at_row = lax.broadcasted_iota(jnp.int32, (cx, count), 0) == (
            site_row[...] >> (cy.bit_length() - 1)
        )
        motion = jnp.concatenate(
            [
                jnp.sum(jnp.where(at_row, cells[c * cx:(c + 1) * cx], 0.0), axis=0, keepdims=True)
                for c in range(ncomp)
            ]
            + [jnp.zeros((8 - ncomp, count), jnp.float32)],
            axis=0,
        )
        outgoing = lax.dot_general(
            motion, placing[...], (((1,), (1,)), ((), ())),
            precision=HIGHEST, preferred_element_type=jnp.float32,
        )
        width = n_gx * capacity
        for y in range(n_gy):
            send_1[y] = outgoing[:, y * width:(y + 1) * width]
        start_hop(hop_1)

    part = n_gy * capacity
    narrow = lax.broadcasted_iota(jnp.int32, (8, LANES), 1)

    def relay_motion():
        end_hop(hop_1)
        for x in range(n_gx):
            tile, start = divmod(x * capacity, LANES)
            total = jnp.zeros((8, LANES), jnp.float32)
            for y in range(n_gy):
                piece = recv_1[y, :, tile * LANES:(tile + 1) * LANES]
                shift = (y * capacity - start) % LANES
                if shift:
                    piece = pltpu.roll(piece, shift, 1)
                here = jnp.logical_and(narrow >= y * capacity, narrow < (y + 1) * capacity)
                total = jnp.where(here, piece, total)
            send_2[x] = total
        start_hop(hop_2)

    def add_forcing():
        end_hop(hop_2)
        per_tile = LANES // part
        for tile in range(slots // LANES):
            total = recv_2[tile * per_tile]
            for i in range(1, per_tile):
                piece = pltpu.roll(recv_2[tile * per_tile + i], i * part, 1)
                total = jnp.where(narrow >= i * part, piece, total)
            moved[:, tile * LANES:(tile + 1) * LANES] = total

        def chunk(i, carry):
            cols = pl.ds(pl.multiple_of(i * LANES, LANES), LANES)
            ids = lax.broadcasted_iota(jnp.int32, (nf, LANES), 0)
            phase = ids - 3 * ((ids * 43691) >> 17)
            m = moved[:, cols]
            force = jnp.where(phase == 0, m[0:1], jnp.where(phase == 1, m[1:2], m[2:3]))
            f_acc[:, cols] = f_acc[:, cols] - force
            f_vel[:, cols] = f_vel[:, cols] - (0.5 * time_step) * force
            return carry

        lax.fori_loop(0, slots // LANES, chunk, 0)
        store(f_acc, acc_out)
        store(f_vel, vel_out)

    for c in range(ncomp):
        now_in[c].wait()
        first_edges(c, 0)
    for c in range(ncomp):
        first_edges(c, 1)
    for copy in field_in:
        copy.wait()
    top_step(0)
    for copy in frames_in:
        copy.wait()
    lax.fori_loop(0, slots // wide, frames, 0)
    store(fd, disp_out)
    store(fh, hyst_out)
    top_step(1)
    locate()
    deep_step(0, 0)
    top_step(2)
    deep_step(0, 1)
    top_step(3)
    post_motion()
    deep_step(0, 2)
    deep_step(1, 0)
    relay_motion()
    deep_step(1, 1)
    deep_step(1, 2)
    deep_step(2, 0)
    store(lev_a.at[0, pl.ds(2, nz)], before_out.at[0])
    add_forcing()
    for c in range(1, ncomp):
        deep_step(2, c)
        store(lev_a.at[c, pl.ds(2, nz)], before_out.at[c])
    for c in range(ncomp):
        deep_step(3, c)
        store(lev_b.at[c, pl.ds(2, nz)], last_out.at[c])
    for k in range(STEPS):
        for c in range(ncomp):
            for t in range(2):
                wait_sent(k, c, t)
    for hop in (hop_1, hop_2):
        for off in range(1, hop[1]):
            parcel(*hop, off, True).wait_send()
    for copy in stores:
        copy.wait()


def shards(
    n_gx, n_gy,
    u_prev, u_now, speeds, sites, routes,
    frame_disp, frame_vel, frame_acc, frame_hyst, frame_kind, stiffness,
):
    ncomp, nz, cx, cy = u_now.shape
    devices = n_gx * n_gy
    nf, slots = frame_disp.shape
    capacity = slots // devices
    count = sites.shape[0]
    f32 = jnp.float32
    i32 = jnp.int32
    field = jax.ShapeDtypeStruct(u_now.shape, f32)
    frame = jax.ShapeDtypeStruct(frame_disp.shape, f32)
    anyspec = pl.BlockSpec(memory_space=pl.ANY)
    level = pltpu.VMEM((ncomp, nz + 4, cx, cy), f32)
    x_edges = pltpu.VMEM((STEPS, ncomp, 2, nz, 2 * cy // LANES, LANES), f32)
    y_edges = pltpu.VMEM((STEPS, ncomp, 2, 2, cx, LANES), f32)
    batch = pltpu.VMEM((nf, slots), f32)
    plane = pltpu.VMEM((ncomp, cx, cy), f32)
    first_hop = pltpu.VMEM((n_gy, 8, n_gx * capacity), f32)
    second_hop = pltpu.VMEM((n_gx, 8, LANES), f32)
    halo_sem = pltpu.SemaphoreType.DMA((STEPS, ncomp, 2, 2))
    return pl.pallas_call(
        functools.partial(wave_kernel, n_gx, n_gy, capacity),
        out_shape=(field, field, frame, frame, frame, frame),
        in_specs=[anyspec] * 11,
        out_specs=(anyspec,) * 6,
        scratch_shapes=[
            level, level, pltpu.VMEM(speeds.shape, f32),
            x_edges, x_edges, y_edges, y_edges,
            batch, batch, batch, batch, pltpu.VMEM(stiffness.shape, f32), batch, batch,
            pltpu.VMEM((1, count), i32), pltpu.VMEM((1, count), i32), pltpu.VMEM((1, slots), i32),
            pltpu.VMEM((cy, count), f32), pltpu.VMEM((slots, count), f32),
            plane, plane, first_hop, first_hop, second_hop, second_hop,
            pltpu.VMEM((8, slots), f32),
            pltpu.SemaphoreType.DMA((2 * ncomp + 9,)),
            pltpu.SemaphoreType.DMA((2 * ncomp + 4,)),
            halo_sem, halo_sem, halo_sem, halo_sem,
            pltpu.SemaphoreType.DMA((n_gy,)), pltpu.SemaphoreType.DMA((n_gy,)),
            pltpu.SemaphoreType.DMA((n_gx,)), pltpu.SemaphoreType.DMA((n_gx,)),
        ],
        compiler_params=pltpu.CompilerParams(
            collective_id=0, has_side_effects=True, vmem_limit_bytes=52 * 1024 * 1024
        ),
        name="wave",
    )(
        u_prev, u_now, speeds, sites.reshape(1, count), routes.reshape(1, count),
        frame_disp, frame_vel, frame_acc, frame_hyst, frame_kind.reshape(1, slots), stiffness,
    )


def solution(mesh):
    cells = P(None, None, "gx", "gy")
    both = ("gx", "gy")
    frame = P(None, both)
    return jax.shard_map(
        functools.partial(shards, mesh.shape["gx"], mesh.shape["gy"]),
        mesh=mesh,
        in_specs=(cells, cells, cells, P(both), P(both, None), frame, frame, frame, frame,
                  P(both), P()),
        out_specs=(cells, cells, frame, frame, frame, frame),
        check_vma=False,
    )
```
